32 devices in a mesh: group: 8 (over y, x, core), tensor: 4 (over z).
Axes of the slice: x: 2, y: 2, z: 4, core: 2. Of those that a mesh axis runs over, the one named last changes fastest.
Arguments:
- hidden: bfloat16 [2048, 4096], P('group'), may hold values from -6 to 6
- w_value: bfloat16 [4096, 512], P('group', 'tensor'), may hold values from -0.09375 to 0.09375
- queries: bfloat16 [2048, 2048], P('group', 'tensor'), may hold values from -12 to 12
- keys: bfloat16 [2048, 512], P('group', 'tensor'), may hold values from -12 to 12
- out_grad: bfloat16 [2048, 2048], P('group', 'tensor'), may hold values from -6 to 6
- lengths: int32 [8, 6], P('group'), may hold values from 1 to 128, 256 in all within a row
Outputs:
- attn_out: bfloat16 [2048, 2048], P('group', 'tensor')
- query_grad: bfloat16 [2048, 2048], P('group', 'tensor')
- key_grad: bfloat16 [2048, 512], P('group', 'tensor')
- input_grad: bfloat16 [2048, 4096], P('group', 'tensor')
- value_weight_grad: float32 [4096, 512], P('group', 'tensor')
The draws below stay inside these ranges and needn't reach their ends.
Inputs may be any that keep to these rules, and one draw needn't show every extreme that they name: Each row of lengths sums to 256, and its largest entry is exactly 128.
All inputs are finite; a program needn't handle non-finite values.
Results may differ from the reference program's by a relative error of at most 0.013.
Values may be sent and summed in bfloat16 or wider, within the bound.
A program may use at most 64 MiB of HBM per device.

```python
import math
from functools import partial
import jax
import jax.numpy as jnp
import numpy as np
from jax import lax

DW = 4096
DH = 128
QPK = 4
TOK_DEV = 256
SEGS = 6
GROUPS = 8
KVH = 4
HQ = 16
TOKENS = 2048


def plant_pattern(key):
    base_key = jax.random.fold_in(key, 303)
    pick_key, sign_key, level_key, margin_key, spot_key = jax.random.split(base_key, 5)
    places = jnp.arange(TOKENS, dtype=jnp.int32)
    chosen = (jax.random.randint(pick_key, (TOKENS,), 0, 8) == 0) & (places % 2 == 1)
    sign_table = (2 * jax.random.randint(sign_key, (TOKENS, KVH, DH), 0, 2) - 1).astype(jnp.float32)
    level_table = jax.random.uniform(level_key, (TOKENS, KVH), jnp.float32, 120.0, 420.0)
    margin_table = jax.random.uniform(margin_key, (TOKENS, KVH), jnp.float32, 1.5, 2.5)
    spot_table = jax.random.randint(spot_key, (TOKENS, KVH), 0, DH)
    scale_root = math.sqrt(DH)
    amplitude = jnp.sqrt(level_table / scale_root)
    bump_height = margin_table * scale_root / amplitude
    return (chosen, sign_table, amplitude, bump_height, spot_table)


def base_noise(key, noise_shape):
    return jnp.clip(jax.random.normal(key, noise_shape, jnp.float32), -6.0, 6.0)


def draw_queries(key, part):
    chosen, sign_table, amplitude, bump_height, spot_table = plant_pattern(key)
    noise = base_noise(jax.random.fold_in(key, 101), (TOKENS, KVH, QPK, DH))
    planted = (amplitude[:, :, None] * sign_table)[:, :, None, :]
    mixed = jnp.where(chosen[:, None, None, None], planted, noise)
    return mixed.reshape(TOKENS, HQ * DH).astype(jnp.bfloat16)


def draw_keys(key, part):
    chosen, sign_table, amplitude, bump_height, spot_table = plant_pattern(key)
    noise = base_noise(jax.random.fold_in(key, 202), (TOKENS, KVH, DH))
    aligned = amplitude[:, :, None] * sign_table
    spot_onehot = (jnp.arange(DH, dtype=jnp.int32)[None, None, :] == spot_table[:, :, None]).astype(jnp.float32)
    own_row = aligned + bump_height[:, :, None] * sign_table * spot_onehot
    next_chosen = jnp.roll(chosen, -1)
    before_row = jnp.roll(aligned, -1, axis=0)
    mixed = jnp.where(chosen[:, None, None], own_row, jnp.where(next_chosen[:, None, None], before_row, noise))
    return mixed.reshape(TOKENS, KVH * DH).astype(jnp.bfloat16)


def block_levels(rng, extent, cuts, low, largest):
    gain = 1.0
    for position, blocks in cuts:
        draws = jax.random.uniform(jax.random.fold_in(jax.random.fold_in(rng, 6), position), (blocks,), jnp.float32, low / len(cuts), largest / len(cuts))
        gain = gain * jnp.repeat(jnp.exp(draws), extent[position] // blocks).reshape((-1,) + (1,) * (len(extent) - 1 - position))
    return gain


def split_up(count, total, reach, lean):
    weights = [(1 << 20) // math.isqrt(standing ** lean) + 1 for standing in range(2, count + 1)]
    surplus, holding = total - reach - (count - 1), [1] * (count - 1)
    while surplus > 0:
        movable = [i for i in range(count - 1) if holding[i] < reach]
        whole, budget = sum([weights[i] for i in movable]), surplus
        for i in movable:
            more = min(reach - holding[i], max(1, budget * weights[i] // whole), surplus)
            holding[i] = holding[i] + more
            surplus = surplus - more
    return np.array([reach] + holding)


def ragged(own_key, count, total, most, skew):
    if count == 2:
        one = jax.random.randint(own_key, (), max(1, total - most), min(most, total - 1) + 1)
        return jnp.stack([one, total - one])
    tallies = jnp.asarray(split_up(count, total, most, skew), jnp.int32)
    pairs = (count - 1) // 2
    donor, taker = tallies[1:1 + 2 * pairs:2], tallies[2:2 + 2 * pairs:2]
    slack = jnp.minimum(donor - 1, most - taker)
    passed = jax.random.randint(jax.random.fold_in(own_key, 1), (pairs,), 0, 1 << 20) % (slack + 1)
    tallies = tallies.at[1:1 + 2 * pairs:2].set(donor - passed).at[2:2 + 2 * pairs:2].set(taker + passed)
    return tallies[jax.random.permutation(jax.random.fold_in(own_key, 2), count)]


def centred(own_key, shape, scale, reach, pieces=(), kind=jnp.bfloat16):
    loudness = block_levels(own_key, shape, pieces, -0.22, 0.18) if pieces else 1.0
    entries = jax.random.normal(own_key, shape, jnp.float32) * scale * loudness
    return jnp.minimum(jnp.maximum(entries, -reach), reach).astype(kind)


def setup_inputs(seed: int = 0) -> dict:
    seeds = jax.random.split(jax.random.key(seed), 7)
    hidden = centred(seeds[0], (TOKENS, DW), 1.0, 6.0, ((0, 8),))
    w_value = centred(seeds[1], (DW, KVH * DH), DW ** -0.5, 0.09375, ((0, 8), (1, 4)))
    queries = draw_queries(jax.random.fold_in(seeds[6], 71), 0)
    keys = draw_keys(jax.random.fold_in(seeds[6], 71), 0)
    out_grad = centred(seeds[4], (TOKENS, HQ * DH), 1.0, 6.0, ((0, 8), (1, 4)))
    lengths = jax.vmap(lambda own: ragged(own, SEGS, TOK_DEV, TOK_DEV // 2, 2))(jax.random.split(seeds[5], GROUPS)).reshape((GROUPS, SEGS)).astype(jnp.int32)
    return {"hidden": hidden, "w_value": w_value, "queries": queries, "keys": keys, "out_grad": out_grad, "lengths": lengths}


def doc_mask(lengths_row):
    bounds = jnp.cumsum(lengths_row).astype(jnp.int32)
    places = jnp.arange(TOK_DEV, dtype=jnp.int32)
    owners = jnp.sum((places[:, None] >= bounds[None, :]).astype(jnp.int32), axis=1)
    return (owners[:, None] == owners[None, :]) & (places[:, None] >= places[None, :])


def attend_group(w_value, operands):
    hidden_rows, query_rows, key_rows, grad_rows, lengths_row = operands
    values = jnp.dot(hidden_rows, w_value, preferred_element_type=jnp.float32).astype(jnp.bfloat16)
    key_heads = key_rows.astype(jnp.float32).reshape(TOK_DEV, KVH, DH)
    value_heads = values.astype(jnp.float32).reshape(TOK_DEV, KVH, DH)
    query_heads = query_rows.astype(jnp.float32).reshape(TOK_DEV, KVH, QPK, DH)
    grad_heads = grad_rows.astype(jnp.float32).reshape(TOK_DEV, KVH, QPK, DH)
    visible = doc_mask(lengths_row)
    score_scale = DH ** -0.5
    scores = jnp.einsum('tkqd,skd->kqts', query_heads, key_heads) * score_scale
    scores = jnp.where(visible, scores, -1e30)
    scores = scores - jnp.max(scores, axis=-1, keepdims=True)
    expons = jnp.exp(scores)
    probs = expons / jnp.sum(expons, axis=-1, keepdims=True)
    probs_low = lax.optimization_barrier(probs.astype(jnp.bfloat16)).astype(jnp.float32)
    output = jnp.einsum('kqts,skd->tkqd', probs_low, value_heads).astype(jnp.bfloat16)
    prob_grad = jnp.einsum('tkqd,skd->kqts', grad_heads, value_heads)
    value_grad = jnp.einsum('kqts,tkqd->skd', probs_low, grad_heads).astype(jnp.bfloat16)
    row_sums = jnp.sum(probs * prob_grad, axis=-1, keepdims=True)
    score_grad = (probs * (prob_grad - row_sums) * score_scale).astype(jnp.bfloat16)
    score_grad = lax.optimization_barrier(score_grad).astype(jnp.float32)
    query_grad = jnp.einsum('kqts,skd->tkqd', score_grad, key_heads).astype(jnp.bfloat16)
    key_grad = jnp.einsum('kqts,tkqd->skd', score_grad, query_heads).astype(jnp.bfloat16)
    value_grad = value_grad.reshape(TOK_DEV, KVH * DH)
    input_sum = jnp.zeros((TOK_DEV, DW), jnp.float32)
    for head_index in range(KVH):
        lower = head_index * DH
        upper = lower + DH
        head_term = jnp.dot(value_grad[:, lower:upper], w_value[:, lower:upper].T, preferred_element_type=jnp.float32)
        input_sum = input_sum + lax.optimization_barrier(head_term.astype(jnp.bfloat16)).astype(jnp.float32)
    return (output.reshape(TOK_DEV, HQ * DH), query_grad.reshape(TOK_DEV, HQ * DH),
            key_grad.reshape(TOK_DEV, KVH * DH), value_grad, input_sum.astype(jnp.bfloat16))


def reference(hidden, w_value, queries, keys, out_grad, lengths):
    grouped = (hidden.reshape(GROUPS, TOK_DEV, DW), queries.reshape(GROUPS, TOK_DEV, HQ * DH),
               keys.reshape(GROUPS, TOK_DEV, KVH * DH), out_grad.reshape(GROUPS, TOK_DEV, HQ * DH), lengths)
    output, query_grad, key_grad, value_grad, input_grad = lax.map(partial(attend_group, w_value), grouped)
    output = output.reshape(TOKENS, HQ * DH)
    query_grad = query_grad.reshape(TOKENS, HQ * DH)
    key_grad = key_grad.reshape(TOKENS, KVH * DH)
    value_grad = value_grad.reshape(TOKENS, KVH * DH)
    input_grad = input_grad.reshape(TOKENS, DW)
    value_weight_grad = jnp.dot(hidden.T, value_grad, preferred_element_type=jnp.float32)
    return output, query_grad, key_grad, input_grad, value_weight_grad
```

```python
import functools

import jax
import jax.numpy as jnp
from jax import lax
from jax.experimental import pallas as pl
from jax.experimental.pallas import tpu as pltpu
from jax.sharding import PartitionSpec as P

MESH = pl.DeviceIdType.MESH
F32 = jnp.float32
BF16 = jnp.bfloat16


def dot(a, b, dims):
    return lax.dot_general(a, b, (dims, ((), ())), preferred_element_type=F32)


def kernel(
    G, T, QPK, SEGS,
    hid_hbm, w_hbm, q_hbm, k_hbm, do_hbm, len_ref,
    out_ref, dq_ref, dk_ref, din_ref, dw_ref,
    hid, wfull, q, k, do, probs, vg, wt, part, acc, rcore, rstage,
    in_sem, ag_s, ag_r, z_s, z_r, sb_s, sb_r, vg_s, vg_r, rc_s, rc_r, rs_s, rs_r,
):
    g, z = lax.axis_index("group"), lax.axis_index("tensor")
    n = G.bit_length() - 1
    top = n - 1
    codes = 1 << top
    rows = wfull.shape[0] // G
    feats = wfull.shape[0] // T
    per = G // T
    tok, dh = k.shape
    core = lax.rem(g, 2)
    flips = [(1 - 2 * lax.rem(g // (1 << j), 2)) * (1 << j) for j in range(n)]
    sib = g + flips[0]

    def step(i, c):
        a, b = flips[i + 1], flips[(i + 1) % top + 1]
        return (1 - c) * a + c * b

    def shift(code, c):
        total = 0
        for i in range(top):
            if code >> i & 1:
                total = total + step(i, c)
        return total

    def wrows(o):
        return pl.ds(pl.multiple_of(o * rows, rows), rows)

    def remote(src, dst, ss, rs, gg, tt):
        return pltpu.make_async_remote_copy(
            src_ref=src, dst_ref=dst, send_sem=ss, recv_sem=rs,
            device_id=(gg, tt), device_id_type=MESH)

    loads = [
        pltpu.make_async_copy(w_hbm, wfull.at[wrows(g)], in_sem.at[0]),
        pltpu.make_async_copy(q_hbm, q, in_sem.at[1]),
        pltpu.make_async_copy(k_hbm, k, in_sem.at[2]),
        pltpu.make_async_copy(do_hbm, do, in_sem.at[3]),
        pltpu.make_async_copy(hid_hbm, hid, in_sem.at[4]),
    ]
    for c in loads:
        c.start()
    barrier = pltpu.get_barrier_semaphore()
    for j in range(n):
        pl.semaphore_signal(barrier, inc=1, device_id=(g + flips[j], z), device_id_type=MESH)
    for r in range(1, T):
        pl.semaphore_signal(barrier, inc=1, device_id=(g, lax.rem(z + r, T)), device_id_type=MESH)
    pl.semaphore_wait(barrier, n + T - 1)

    def ag_copy(code, i):
        o = wfull.at[wrows(g + shift(code, core))]
        to = sib if i == top else g + step(i, core)
        new = code | 1 << i
        return remote(o, o, ag_s.at[new], ag_r.at[new], to, z)

    def z_copy(code):
        o = g + shift(code, core)
        tt, b = o // per, lax.rem(o, per)
        return tt, remote(
            wfull.at[wrows(o)],
            wt.at[pl.ds(pl.multiple_of(b * rows, rows), rows), pl.ds(pl.multiple_of(z * dh, dh), dh)],
            z_s.at[code], z_r.at[z, b], g, tt)

    sends = []

    def spread(code):
        for i in range(top):
            if code >> i == 0:
                c = ag_copy(code, i)
                c.start()
                sends.append(c)
        tt, zc = z_copy(code)

        @pl.when(tt != z)
        def _():
            zc.start()

        c = ag_copy(code, top)
        c.start()
        sends.append(c)

    def ag_wait(new):
        if new >> top & 1:
            o = sib + shift(new & (codes - 1), 1 - core)
        else:
            o = g + shift(new, core)
        r = wfull.at[wrows(o)]
        remote(r, r, ag_s.at[new], ag_r.at[new], sib, z).wait_recv()

    loads[0].wait()
    spread(0)

    loads[1].wait()
    loads[2].wait()
    loads[3].wait()
    ti = lax.broadcasted_iota(jnp.int32, (tok, 1), 0)
    si = lax.broadcasted_iota(jnp.int32, (1, tok), 1)
    ot, os_, bound = jnp.zeros_like(ti), jnp.zeros_like(si), 0
    for i in range(SEGS):
        bound = bound + len_ref[0, i]
        ot = ot + (ti >= bound).astype(jnp.int32)
        os_ = os_ + (si >= bound).astype(jnp.int32)
    visible = (ot == os_) & (ti >= si)
    scale = dh ** (-0.5)
    kk = k[...]
    vgt = jnp.zeros((dh, tok), F32)
    for j in range(QPK):
        s = dot(q[:, j * dh:(j + 1) * dh], kk, ((1,), (1,))) * scale
        s = jnp.where(visible, s, -1e30)
        e = jnp.exp(s - jnp.max(s, axis=-1, keepdims=True))
        p = e / jnp.sum(e, axis=-1, keepdims=True)
        probs[j] = p
        vgt = vgt + dot(do[:, j * dh:(j + 1) * dh], p.astype(BF16), ((0,), (0,)))
    vgb = vgt.T.astype(BF16)
    mine = pl.ds(pl.multiple_of(z * dh, dh), dh)
    vg[:, mine] = vgb

    def vg_copy(r):
        return remote(vg.at[:, mine], vg.at[:, mine], vg_s.at[r], vg_r.at[z],
                      g, lax.rem(z + r, T))

    for r in range(1, T):
        c = vg_copy(r)
        c.start()
        sends.append(c)

    loads[4].wait()
    width = min(512, hid.shape[1])
    for b in range(hid.shape[1] // width):
        x = dot(hid[:, b * width:(b + 1) * width], vgb, ((0,), (0,)))
        part[b * width:(b + 1) * width, :] = x.astype(BF16)
    for code in reversed(range(codes)):
        c = remote(part.at[wrows(sib + shift(code, 1 - core))], rcore.at[code],
                   rc_s.at[code], rc_r.at[code], sib, z)
        c.start()
        sends.append(c)

    relay = sorted(range(1, codes), key=lambda v: (bin(v).count("1"), v))
    for code in relay[:-1]:
        ag_wait(code)
        spread(code)

    def core_add(code):
        remote(rcore.at[code], rcore.at[code], rc_s.at[code], rc_r.at[code], sib, z).wait_recv()
        own = part[wrows(g + shift(code, core)), :].astype(F32)
        acc[code] = (own + rcore[code].astype(F32)).astype(BF16)

    def stage_copy(p, low):
        at = (1 << p) + low
        return remote(acc.at[at], rstage.at[at], rs_s.at[at], rs_r.at[at], g + step(p, core), z)

    def stage_send(p):
        for low in range(1 << p):
            c = stage_copy(p, low)
            c.start()
            sends.append(c)

    def stage_add(p):
        for low in range(1 << p):
            at = (1 << p) + low
            stage_copy(p, low).wait_recv()
            total = acc[low].astype(F32) + rstage[at].astype(F32)
            if p == 0:
                dw_ref[...] = total
            else:
                acc[low] = total.astype(BF16)

    for code in reversed(range(codes >> 1, codes)):
        core_add(code)
    stage_send(top - 1)
    for code in reversed(range(codes >> 1)):
        core_add(code)
    for code in relay[-1:]:
        ag_wait(code)
        spread(code)
    for p in reversed(range(1, top)):
        stage_add(p)
        stage_send(p - 1)

    for code in range(codes, 2 * codes):
        ag_wait(code)
    values = dot(hid[...], wfull[...], ((1,), (0,))).astype(BF16)
    dkt = jnp.zeros((dh, tok), F32)
    for j in range(QPK):
        cols = slice(j * dh, (j + 1) * dh)
        p = probs[j]
        pb = p.astype(BF16)
        out_ref[:, cols] = dot(pb, values, ((1,), (0,))).astype(BF16)
        dp = dot(do[:, cols], values, ((1,), (1,)))
        rs = jnp.sum(p * dp, axis=-1, keepdims=True)
        ds = (p * (dp - rs) * scale).astype(BF16)
        dq_ref[:, cols] = dot(ds, kk, ((1,), (0,))).astype(BF16)
        dkt = dkt + dot(q[:, cols], ds, ((0,), (0,)))
    dk_ref[...] = dkt.T.astype(BF16)
    stage_add(0)

    def block(b, head):
        return wt.at[pl.ds(pl.multiple_of(b * rows, rows), rows),
                     pl.ds(pl.multiple_of(head * dh, dh), dh)]

    for i in range(per // 2):
        for r in range(1, T):
            head, b = lax.rem(z + r, T), 2 * i + core
            ref = block(b, head)
            remote(ref, ref, z_s.at[0], z_r.at[head, b], g, head).wait_recv()
            c = remote(ref, ref, sb_s.at[i, r], sb_r.at[i, r], sib, z)
            c.start()
            sends.append(c)
    wt[:, mine] = wfull[pl.ds(pl.multiple_of(z * feats, feats), feats), :]
    for r in range(1, T):
        head = lax.rem(z + r, T)
        ref = vg.at[:, pl.ds(pl.multiple_of(head * dh, dh), dh)]
        remote(ref, ref, vg_s.at[r], vg_r.at[head], g, head).wait_recv()
    for i in range(per // 2):
        for r in range(1, T):
            ref = block(2 * i + 1 - core, lax.rem(z + r, T))
            remote(ref, ref, sb_s.at[i, r], sb_r.at[i, r], sib, z).wait_recv()
    din_ref[...] = dot(vg[...], wt[...], ((1,), (1,))).astype(BF16)
    for c in sends:
        c.wait_send()
    for code in range(codes):
        tt, zc = z_copy(code)

        @pl.when(tt != z)
        def _():
            zc.wait_send()


def per_device(G, T, hidden, w_value, queries, keys, out_grad, lengths):
    tok, dw = hidden.shape
    rows, dh = w_value.shape
    qpk = queries.shape[1] // dh
    codes = G // 2
    sds = jax.ShapeDtypeStruct
    dma = pltpu.SemaphoreType.DMA
    any_spec = pl.BlockSpec(memory_space=pl.ANY)
    vmem = pl.BlockSpec(memory_space=pltpu.VMEM)
    return pl.pallas_call(
        functools.partial(kernel, G, T, qpk, lengths.shape[1]),
        out_shape=(
            sds(queries.shape, BF16), sds(queries.shape, BF16), sds(keys.shape, BF16),
            sds((tok, dw // T), BF16), sds(w_value.shape, F32),
        ),
        in_specs=[any_spec] * 5 + [pl.BlockSpec(memory_space=pltpu.SMEM)],
        out_specs=(vmem,) * 5,
        scratch_shapes=[
            pltpu.VMEM((tok, dw), BF16),
            pltpu.VMEM((dw, dh), BF16),
            pltpu.VMEM(queries.shape, BF16),
            pltpu.VMEM(keys.shape, BF16),
            pltpu.VMEM(queries.shape, BF16),
            pltpu.VMEM((qpk, tok, tok), F32),
            pltpu.VMEM((tok, T * dh), BF16),
            pltpu.VMEM((dw // T, T * dh), BF16),
            pltpu.VMEM((dw, dh), BF16),
            pltpu.VMEM((codes, rows, dh), BF16),
            pltpu.VMEM((codes, rows, dh), BF16),
            pltpu.VMEM((codes, rows, dh), BF16),
            dma((5,)),
            dma((G,)), dma((G,)),
            dma((codes,)), dma((T, G // T)),
            dma((G // T // 2, T)), dma((G // T // 2, T)),
            dma((T,)), dma((T,)),
            dma((codes,)), dma((codes,)),
            dma((codes,)), dma((codes,)),
        ],
        compiler_params=pltpu.CompilerParams(
            collective_id=0, has_side_effects=True, vmem_limit_bytes=40 * 1024 * 1024),
    )(hidden, w_value, queries, keys, out_grad, lengths)


def solution(mesh):
    row, both = P("group", None), P("group", "tensor")
    return jax.shard_map(
        functools.partial(per_device, mesh.shape["group"], mesh.shape["tensor"]),
        mesh=mesh,
        in_specs=(row, both, both, both, both, row),
        out_specs=(both,) * 5,
        check_vma=False,
    )
```

```python
import functools

import jax
import jax.numpy as jnp
from jax import lax
from jax.experimental import pallas as pl
from jax.experimental.pallas import tpu as pltpu
from jax.sharding import PartitionSpec as P

MESH = pl.DeviceIdType.MESH
F32 = jnp.float32
BF16 = jnp.bfloat16


def dot(a, b, dims):
    return lax.dot_general(a, b, (dims, ((), ())), preferred_element_type=F32)


def kernel(
    G, T, QPK, SEGS,
    hid_hbm, w_hbm, q_hbm, k_hbm, do_hbm, len_hbm,
    out_ref, dq_ref, dk_ref, din_ref, dw_ref,
    lens, hid, wfull, q, k, do, probs, vg, wt, part, acc, rcore, rstage,
    in_sem, ag_s, ag_r, z_s, z_r, sb_s, sb_r, vg_s, vg_r, rc_s, rc_r, rs_s, rs_r,
):
    g, z = lax.axis_index("group"), lax.axis_index("tensor")
    n = G.bit_length() - 1
    top = n - 1
    codes = 1 << top
    rows = wfull.shape[0] // G
    feats = wfull.shape[0] // T
    per = G // T
    tok, dh = k.shape
    core = lax.rem(g, 2)
    flips = [(1 - 2 * lax.rem(g // (1 << j), 2)) * (1 << j) for j in range(n)]
    sib = g + flips[0]

    def step(i, c):
        a, b = flips[i + 1], flips[(i + 1) % top + 1]
        return (1 - c) * a + c * b

    def shift(code, c):
        total = 0
        for i in range(top):
            if code >> i & 1:
                total = total + step(i, c)
        return total

    def wrows(o):
        return pl.ds(pl.multiple_of(o * rows, rows), rows)

    def remote(src, dst, ss, rs, gg, tt):
        return pltpu.make_async_remote_copy(
            src_ref=src, dst_ref=dst, send_sem=ss, recv_sem=rs,
            device_id=(gg, tt), device_id_type=MESH)

    loads = [
        pltpu.make_async_copy(w_hbm, wfull.at[wrows(g)], in_sem.at[0]),
        pltpu.make_async_copy(q_hbm, q, in_sem.at[1]),
        pltpu.make_async_copy(k_hbm, k, in_sem.at[2]),
        pltpu.make_async_copy(do_hbm, do, in_sem.at[3]),
        pltpu.make_async_copy(hid_hbm, hid, in_sem.at[4]),
        pltpu.make_async_copy(len_hbm, lens, in_sem.at[5]),
    ]
    for c in loads:
        c.start()
    barrier = pltpu.get_barrier_semaphore()
    for j in range(n):
        pl.semaphore_signal(barrier, inc=1, device_id=(g + flips[j], z), device_id_type=MESH)
    for r in range(1, T):
        pl.semaphore_signal(barrier, inc=1, device_id=(g, lax.rem(z + r, T)), device_id_type=MESH)
    pl.semaphore_wait(barrier, n + T - 1)

    def ag_copy(code, i):
        o = wfull.at[wrows(g + shift(code, core))]
        to = sib if i == top else g + step(i, core)
        new = code | 1 << i
        return remote(o, o, ag_s.at[new], ag_r.at[new], to, z)

    def z_copy(code):
        o = g + shift(code, core)
        tt, b = o // per, lax.rem(o, per)
        return tt, remote(
            wfull.at[wrows(o)],
            wt.at[pl.ds(pl.multiple_of(b * rows, rows), rows), pl.ds(pl.multiple_of(z * dh, dh), dh)],
            z_s.at[code], z_r.at[z, b], g, tt)

    sends = []

    def spread(code):
        for i in range(top):
            if code >> i == 0:
                c = ag_copy(code, i)
                c.start()
                sends.append(c)
        tt, zc = z_copy(code)

        @pl.when(tt != z)
        def _():
            zc.start()

        c = ag_copy(code, top)
        c.start()
        sends.append(c)

    def ag_wait(new):
        if new >> top & 1:
            o = sib + shift(new & (codes - 1), 1 - core)
        else:
            o = g + shift(new, core)
        r = wfull.at[wrows(o)]
        remote(r, r, ag_s.at[new], ag_r.at[new], sib, z).wait_recv()

    loads[0].wait()
    spread(0)

    loads[1].wait()
    loads[2].wait()
    loads[3].wait()
    loads[5].wait()
    ti = lax.broadcasted_iota(jnp.int32, (tok, 1), 0)
    si = lax.broadcasted_iota(jnp.int32, (1, tok), 1)
    ot, os_, bound = jnp.zeros_like(ti), jnp.zeros_like(si), 0
    for i in range(SEGS):
        bound = bound + lens[0, i]
        ot = ot + (ti >= bound).astype(jnp.int32)
        os_ = os_ + (si >= bound).astype(jnp.int32)
    visible = (ot == os_) & (ti >= si)
    scale = dh ** (-0.5)
    kk = k[...]
    vgt = jnp.zeros((dh, tok), F32)
    for j in range(QPK):
        s = dot(q[:, j * dh:(j + 1) * dh], kk, ((1,), (1,))) * scale
        s = jnp.where(visible, s, -1e30)
        e = jnp.exp(s - jnp.max(s, axis=-1, keepdims=True))
        p = e / jnp.sum(e, axis=-1, keepdims=True)
        probs[j] = p
        vgt = vgt + dot(do[:, j * dh:(j + 1) * dh], p.astype(BF16), ((0,), (0,)))
    vgb = vgt.T.astype(BF16)
    mine = pl.ds(pl.multiple_of(z * dh, dh), dh)
    vg[:, mine] = vgb

    def vg_copy(r):
        return remote(vg.at[:, mine], vg.at[:, mine], vg_s.at[r], vg_r.at[z],
                      g, lax.rem(z + r, T))

    for r in range(1, T):
        c = vg_copy(r)
        c.start()
        sends.append(c)

    loads[4].wait()
    width = min(512, hid.shape[1])
    for b in range(hid.shape[1] // width):
        x = dot(hid[:, b * width:(b + 1) * width], vgb, ((0,), (0,)))
        part[b * width:(b + 1) * width, :] = x.astype(BF16)
    for code in reversed(range(codes)):
        c = remote(part.at[wrows(sib + shift(code, 1 - core))], rcore.at[code],
                   rc_s.at[code], rc_r.at[code], sib, z)
        c.start()
        sends.append(c)

    relay = sorted(range(1, codes), key=lambda v: (bin(v).count("1"), v))
    for code in relay[:-1]:
        ag_wait(code)
        spread(code)

    def core_add(code):
        remote(rcore.at[code], rcore.at[code], rc_s.at[code], rc_r.at[code], sib, z).wait_recv()
        own = part[wrows(g + shift(code, core)), :].astype(F32)
        acc[code] = (own + rcore[code].astype(F32)).astype(BF16)

    def stage_copy(p, low):
        at = (1 << p) + low
        return remote(acc.at[at], rstage.at[at], rs_s.at[at], rs_r.at[at], g + step(p, core), z)

    def stage_send(p):
        for low in range(1 << p):
            c = stage_copy(p, low)
            c.start()
            sends.append(c)

    def stage_add(p):
        for low in range(1 << p):
            at = (1 << p) + low
            stage_copy(p, low).wait_recv()
            total = acc[low].astype(F32) + rstage[at].astype(F32)
            if p == 0:
                dw_ref[...] = total
            else:
                acc[low] = total.astype(BF16)

    for code in reversed(range(codes >> 1, codes)):
        core_add(code)
    stage_send(top - 1)
    for code in reversed(range(codes >> 1)):
        core_add(code)
    for code in relay[-1:]:
        ag_wait(code)
        spread(code)
    for p in reversed(range(1, top)):
        stage_add(p)
        stage_send(p - 1)

    for code in range(codes, 2 * codes):
        ag_wait(code)
    values = dot(hid[...], wfull[...], ((1,), (0,))).astype(BF16)
    dkt = jnp.zeros((dh, tok), F32)
    for j in range(QPK):
        cols = slice(j * dh, (j + 1) * dh)
        p = probs[j]
        pb = p.astype(BF16)
        out_ref[:, cols] = dot(pb, values, ((1,), (0,))).astype(BF16)
        dp = dot(do[:, cols], values, ((1,), (1,)))
        rs = jnp.sum(p * dp, axis=-1, keepdims=True)
        ds = (p * (dp - rs) * scale).astype(BF16)
        dq_ref[:, cols] = dot(ds, kk, ((1,), (0,))).astype(BF16)
        dkt = dkt + dot(q[:, cols], ds, ((0,), (0,)))
    dk_ref[...] = dkt.T.astype(BF16)
    stage_add(0)

    def block(b, head):
        return wt.at[pl.ds(pl.multiple_of(b * rows, rows), rows),
                     pl.ds(pl.multiple_of(head * dh, dh), dh)]

    for i in range(per // 2):
        for r in range(1, T):
            head, b = lax.rem(z + r, T), 2 * i + core
            ref = block(b, head)
            remote(ref, ref, z_s.at[0], z_r.at[head, b], g, head).wait_recv()
            c = remote(ref, ref, sb_s.at[i, r], sb_r.at[i, r], sib, z)
            c.start()
            sends.append(c)
    wt[:, mine] = wfull[pl.ds(pl.multiple_of(z * feats, feats), feats), :]
    for r in range(1, T):
        head = lax.rem(z + r, T)
        ref = vg.at[:, pl.ds(pl.multiple_of(head * dh, dh), dh)]
        remote(ref, ref, vg_s.at[r], vg_r.at[head], g, head).wait_recv()
    for i in range(per // 2):
        for r in range(1, T):
            ref = block(2 * i + 1 - core, lax.rem(z + r, T))
            remote(ref, ref, sb_s.at[i, r], sb_r.at[i, r], sib, z).wait_recv()
    din_ref[...] = dot(vg[...], wt[...], ((1,), (1,))).astype(BF16)
    for c in sends:
        c.wait_send()
    for code in range(codes):
        tt, zc = z_copy(code)

        @pl.when(tt != z)
        def _():
            zc.wait_send()


def put_out(count, *refs):
    copies = [
        pltpu.make_async_copy(refs[i], refs[count + i], refs[-1].at[i]) for i in range(count)
    ]
    for c in copies:
        c.start()
    for c in copies:
        c.wait()


def per_device(G, T, hidden, w_value, queries, keys, out_grad, lengths):
    tok, dw = hidden.shape
    rows, dh = w_value.shape
    qpk = queries.shape[1] // dh
    codes = G // 2
    sds = jax.ShapeDtypeStruct
    dma = pltpu.SemaphoreType.DMA
    hbm = pl.BlockSpec(memory_space=pltpu.HBM)
    vmem = pl.BlockSpec(memory_space=pltpu.VMEM)
    results = pl.pallas_call(
        functools.partial(kernel, G, T, qpk, lengths.shape[1]),
        out_shape=(
            pltpu.VMEM(queries.shape, BF16), pltpu.VMEM(queries.shape, BF16), pltpu.VMEM(keys.shape, BF16),
            pltpu.VMEM((tok, dw // T), BF16), pltpu.VMEM(w_value.shape, F32),
        ),
        in_specs=[hbm] * 6,
        out_specs=(vmem,) * 5,
        scratch_shapes=[
            pltpu.SMEM(lengths.shape, jnp.int32),
            pltpu.VMEM((tok, dw), BF16),
            pltpu.VMEM((dw, dh), BF16),
            pltpu.VMEM(queries.shape, BF16),
            pltpu.VMEM(keys.shape, BF16),
            pltpu.VMEM(queries.shape, BF16),
            pltpu.VMEM((qpk, tok, tok), F32),
            pltpu.VMEM((tok, T * dh), BF16),
            pltpu.VMEM((dw // T, T * dh), BF16),
            pltpu.VMEM((dw, dh), BF16),
            pltpu.VMEM((codes, rows, dh), BF16),
            pltpu.VMEM((codes, rows, dh), BF16),
            pltpu.VMEM((codes, rows, dh), BF16),
            dma((6,)),
            dma((G,)), dma((G,)),
            dma((codes,)), dma((T, G // T)),
            dma((G // T // 2, T)), dma((G // T // 2, T)),
            dma((T,)), dma((T,)),
            dma((codes,)), dma((codes,)),
            dma((codes,)), dma((codes,)),
        ],
        compiler_params=pltpu.CompilerParams(
            collective_id=0, has_side_effects=True, vmem_limit_bytes=40 * 1024 * 1024),
    )(*[pltpu.with_memory_space_constraint(x, pltpu.HBM) for x in (hidden, w_value, queries, keys, out_grad, lengths)])
    count = len(results)
    return pl.pallas_call(
        functools.partial(put_out, count),
        out_shape=tuple(sds(x.shape, x.dtype) for x in results),
        in_specs=[pl.BlockSpec(memory_space=pltpu.VMEM)] * count,
        out_specs=(hbm,) * count,
        scratch_shapes=[dma((count,))],
        compiler_params=pltpu.CompilerParams(vmem_limit_bytes=8 * 1024 * 1024),
    )(*results)


def solution(mesh):
    row, both = P("group", None), P("group", "tensor")
    return jax.shard_map(
        functools.partial(per_device, mesh.shape["group"], mesh.shape["tensor"]),
        mesh=mesh,
        in_specs=(row, both, both, both, both, row),
        out_specs=(both,) * 5,
        check_vma=False,
    )
```

```python
import functools

import jax
import jax.numpy as jnp
from jax import lax
from jax.experimental import pallas as pl
from jax.experimental.pallas import tpu as pltpu
from jax.sharding import PartitionSpec as P

FOLD = 1
MESH = pl.DeviceIdType.MESH
F32 = jnp.float32
BF16 = jnp.bfloat16


def dot(a, b, dims):
    return lax.dot_general(a, b, (dims, ((), ())), preferred_element_type=F32)


def kernel(
    G, T, QPK, SEGS, fold,
    hid_hbm, w_hbm, q_hbm, k_hbm, do_hbm, len_hbm,
    out_ref, dq_ref, dk_ref, din_ref, dw_ref,
    lens, hid, wfull, q, k, do, probs, vg, wt, part, acc, rcore, rstage,
    in_sem, ag_s, ag_r, z_s, z_r, w2_s, w2_r, vg_s, vg_r, rc_s, rc_r, rs_s, rs_r,
):
    g, z = lax.axis_index("group"), lax.axis_index("tensor")
    n = G.bit_length() - 1
    top = n - 1
    codes = 1 << top
    rows = wfull.shape[0] // G
    feats = wfull.shape[0] // T
    per = G // T
    tok, dh = k.shape
    core = lax.rem(g, 2)
    flips = [(1 - 2 * lax.rem(g // (1 << j), 2)) * (1 << j) for j in range(n)]
    sib = g + flips[0]

    def step(i, c):
        a, b = flips[i + 1], flips[(i + 1) % top + 1]
        return (1 - c) * a + c * b

    def shift(code, c):
        total = 0
        for i in range(top):
            if code >> i & 1:
                total = total + step(i, c)
        return total

    half = rows // 2
    share = 1 << fold
    size = half // share

    def piece(code, v):
        total = 0
        for i in range(fold):
            bit = lax.rem(g // (1 << ((i + v) % top + 1)), 2)
            total = total + (1 - bit if code >> i & 1 else bit) * (1 << i)
        return total

    def wrows(o):
        return pl.ds(pl.multiple_of(o * rows, rows), rows)

    def prows(o, v, which):
        return pl.ds(pl.multiple_of(o * rows + v * half + which * size, size), size)

    def hrows(o, v):
        return pl.ds(pl.multiple_of(o * rows + v * half, half), half)

    def remote(src, dst, ss, rs, gg, tt):
        return pltpu.make_async_remote_copy(
            src_ref=src, dst_ref=dst, send_sem=ss, recv_sem=rs,
            device_id=(gg, tt), device_id_type=MESH)

    loads = [
        pltpu.make_async_copy(w_hbm, wfull.at[wrows(g)], in_sem.at[0]),
        pltpu.make_async_copy(q_hbm, q, in_sem.at[1]),
        pltpu.make_async_copy(k_hbm, k, in_sem.at[2]),
        pltpu.make_async_copy(do_hbm, do, in_sem.at[3]),
        pltpu.make_async_copy(hid_hbm, hid, in_sem.at[4]),
        pltpu.make_async_copy(len_hbm, lens, in_sem.at[5]),
    ]
    for c in loads:
        c.start()
    barrier = pltpu.get_barrier_semaphore()
    for j in range(n):
        pl.semaphore_signal(barrier, inc=1, device_id=(g + flips[j], z), device_id_type=MESH)
    for r in range(1, T):
        pl.semaphore_signal(barrier, inc=1, device_id=(g, lax.rem(z + r, T)), device_id_type=MESH)
    pl.semaphore_wait(barrier, n + T - 1)

    def ag_copy(v, code, i):
        o = wfull.at[hrows(g + shift(code, v), v)]
        to = sib if i == top else g + step(i, v)
        new = code | 1 << i
        return remote(o, o, ag_s.at[v, new], ag_r.at[v, new], to, z)

    def block(b, v, which, head):
        return wt.at[prows(b, v, which), pl.ds(pl.multiple_of(head * dh, dh), dh)]

    def z_copy(v, code):
        o = g + shift(code, v)
        tt, b = o // per, lax.rem(o, per)
        return tt, remote(wfull.at[prows(o, v, piece(0, v))], block(b, v, piece(0, v), z),
                          z_s.at[v, code], z_r.at[v, z, b], g, tt)

    sends = []

    def pieces_ref(i, r, v, code, c):
        return block(2 * i + c, v, piece(code, v), lax.rem(z + r, T))

    def pieces_send(i, r, v, code, to, new):
        ref = pieces_ref(i, r, v, code, core)
        c = remote(ref, ref, w2_s.at[v, i, r, new], w2_r.at[v, i, r, new], to, z)
        c.start()
        sends.append(c)

    def pieces_wait(i, r, v, new):
        ref = pieces_ref(i, r, v, new % share, 1 - core if new >> fold else core)
        remote(ref, ref, w2_s.at[v, i, r, new], w2_r.at[v, i, r, new], sib, z).wait_recv()

    def pieces(code):
        for i in range(per // 2):
            for r in range(1, T):
                for v in range(2):
                    if code == 0:
                        head, b = lax.rem(z + r, T), 2 * i + core
                        ref = pieces_ref(i, r, v, 0, core)
                        remote(ref, ref, z_s.at[v, 0], z_r.at[v, head, b], g, head).wait_recv()
                    else:
                        pieces_wait(i, r, v, code)
                    for p in range(fold):
                        if code >> p == 0:
                            pieces_send(i, r, v, code, g + step(p, v), code | 1 << p)
                    pieces_send(i, r, v, code, sib, code | share)


    def spread(v, code):
        for i in range(top):
            if code >> i == 0:
                c = ag_copy(v, code, i)
                c.start()
                sends.append(c)
        tt, zc = z_copy(v, code)

        @pl.when(tt != z)
        def _():
            zc.start()

        c = ag_copy(v, code, top)
        c.start()
        sends.append(c)

    def ag_wait(v, new):
        r = wfull.at[hrows((sib if new >> top else g) + shift(new & (codes - 1), v), v)]
        remote(r, r, ag_s.at[v, new], ag_r.at[v, new], sib, z).wait_recv()

    loads[0].wait()
    for v in range(2):
        spread(v, 0)

    loads[1].wait()
    loads[2].wait()
    loads[3].wait()
    loads[5].wait()
    ti = lax.broadcasted_iota(jnp.int32, (tok, 1), 0)
    si = lax.broadcasted_iota(jnp.int32, (1, tok), 1)
    ot, os_, bound = jnp.zeros_like(ti), jnp.zeros_like(si), 0
    for i in range(SEGS):
        bound = bound + lens[0, i]
        ot = ot + (ti >= bound).astype(jnp.int32)
        os_ = os_ + (si >= bound).astype(jnp.int32)
    visible = (ot == os_) & (ti >= si)
    scale = dh ** (-0.5)
    kk = k[...]
    vgt = jnp.zeros((dh, tok), F32)
    for j in range(QPK):
        s = dot(q[:, j * dh:(j + 1) * dh], kk, ((1,), (1,))) * scale
        s = jnp.where(visible, s, -1e30)
        e = jnp.exp(s - jnp.max(s, axis=-1, keepdims=True))
        p = e / jnp.sum(e, axis=-1, keepdims=True)
        probs[j] = p
        vgt = vgt + dot(do[:, j * dh:(j + 1) * dh], p.astype(BF16), ((0,), (0,)))
    vgb = vgt.T.astype(BF16)
    mine = pl.ds(pl.multiple_of(z * dh, dh), dh)
    vg[:, mine] = vgb

    def vg_copy(r):
        return remote(vg.at[:, mine], vg.at[:, mine], vg_s.at[r], vg_r.at[z],
                      g, lax.rem(z + r, T))

    for r in range(1, T):
        c = vg_copy(r)
        c.start()
        sends.append(c)

    loads[4].wait()
    width = min(512, hid.shape[1])
    for b in range(hid.shape[1] // width):
        x = dot(hid[:, b * width:(b + 1) * width], vgb, ((0,), (0,)))
        part[b * width:(b + 1) * width, :] = x.astype(BF16)
    for code in reversed(range(codes)):
        for v in range(2):
            c = remote(part.at[hrows(sib + shift(code, v), v)], rcore.at[v, code],
                       rc_s.at[v, code], rc_r.at[v, code], sib, z)
            c.start()
            sends.append(c)

    relay = sorted(range(1, codes), key=lambda x: (bin(x).count("1"), x))
    for code in relay[:-1]:
        for v in range(2):
            ag_wait(v, code)
            spread(v, code)

    def core_add(v, code):
        ref = rcore.at[v, code]
        remote(ref, ref, rc_s.at[v, code], rc_r.at[v, code], sib, z).wait_recv()
        own = part[hrows(g + shift(code, v), v), :].astype(F32)
        acc[v, code] = (own + rcore[v, code].astype(F32)).astype(BF16)

    def stage_copy(v, p, low):
        at = (1 << p) + low
        return remote(acc.at[v, at], rstage.at[v, at], rs_s.at[v, at], rs_r.at[v, at],
                      g + step(p, v), z)

    def stage_send(p):
        for low in reversed(range(1 << p)):
            for v in range(2):
                c = stage_copy(v, p, low)
                c.start()
                sends.append(c)

    def stage_add(p, span):
        for low in reversed(span):
            for v in range(2):
                stage_copy(v, p, low).wait_recv()
                total = acc[v, low].astype(F32) + rstage[v, (1 << p) + low].astype(F32)
                if p == 0:
                    dw_ref[v * half:(v + 1) * half, :] = total
                else:
                    acc[v, low] = total.astype(BF16)

    for code in reversed(range(codes >> 1, codes)):
        for v in range(2):
            core_add(v, code)
    stage_send(top - 1)
    for code in reversed(range(codes >> 1)):
        for v in range(2):
            core_add(v, code)
    for code in relay[-1:]:
        for v in range(2):
            ag_wait(v, code)
            spread(v, code)
    for p in reversed(range(1, top)):
        middle = 1 << (p - 1)
        stage_add(p, range(middle, 2 * middle))
        stage_send(p - 1)
        stage_add(p, range(middle))

    pieces(0)

    for code in range(codes, 2 * codes):
        for v in range(2):
            ag_wait(v, code)
    values = dot(hid[...], wfull[...], ((1,), (0,))).astype(BF16)
    dkt = jnp.zeros((dh, tok), F32)
    for j in range(QPK):
        cols = slice(j * dh, (j + 1) * dh)
        p = probs[j]
        pb = p.astype(BF16)
        out_ref[:, cols] = dot(pb, values, ((1,), (0,))).astype(BF16)
        dp = dot(do[:, cols], values, ((1,), (1,)))
        rs = jnp.sum(p * dp, axis=-1, keepdims=True)
        ds = (p * (dp - rs) * scale).astype(BF16)
        dq_ref[:, cols] = dot(ds, kk, ((1,), (0,))).astype(BF16)
        dkt = dkt + dot(q[:, cols], ds, ((0,), (0,)))
    dk_ref[...] = dkt.T.astype(BF16)
    stage_add(0, range(1))

    for code in sorted(range(1, share), key=lambda x: (bin(x).count("1"), x)):
        pieces(code)
    wt[:, mine] = wfull[pl.ds(pl.multiple_of(z * feats, feats), feats), :]
    for r in range(1, T):
        head = lax.rem(z + r, T)
        ref = vg.at[:, pl.ds(pl.multiple_of(head * dh, dh), dh)]
        remote(ref, ref, vg_s.at[r], vg_r.at[head], g, head).wait_recv()
    for new in range(share, 2 * share):
        for i in range(per // 2):
            for r in range(1, T):
                for v in range(2):
                    pieces_wait(i, r, v, new)
    din_ref[...] = dot(vg[...], wt[...], ((1,), (1,))).astype(BF16)
    for c in sends:
        c.wait_send()
    for code in range(codes):
        for v in range(2):
            tt, zc = z_copy(v, code)

            @pl.when(tt != z)
            def _():
                zc.wait_send()


def put_out(count, *refs):
    copies = [
        pltpu.make_async_copy(refs[i], refs[count + i], refs[-1].at[i]) for i in range(count)
    ]
    for c in copies:
        c.start()
    for c in copies:
        c.wait()


def per_device(G, T, hidden, w_value, queries, keys, out_grad, lengths):
    tok, dw = hidden.shape
    rows, dh = w_value.shape
    qpk = queries.shape[1] // dh
    codes = G // 2
    fold = max(0, min(FOLD, codes.bit_length() - 1, (rows // 32).bit_length() - 1))
    sds = jax.ShapeDtypeStruct
    dma = pltpu.SemaphoreType.DMA
    hbm = pl.BlockSpec(memory_space=pltpu.HBM)
    vmem = pl.BlockSpec(memory_space=pltpu.VMEM)
    results = pl.pallas_call(
        functools.partial(kernel, G, T, qpk, lengths.shape[1], fold),
        out_shape=(
            pltpu.VMEM(queries.shape, BF16), pltpu.VMEM(queries.shape, BF16), pltpu.VMEM(keys.shape, BF16),
            pltpu.VMEM((tok, dw // T), BF16), pltpu.VMEM(w_value.shape, F32),
        ),
        in_specs=[hbm] * 6,
        out_specs=(vmem,) * 5,
        scratch_shapes=[
            pltpu.SMEM(lengths.shape, jnp.int32),
            pltpu.VMEM((tok, dw), BF16),
            pltpu.VMEM((dw, dh), BF16),
            pltpu.VMEM(queries.shape, BF16),
            pltpu.VMEM(keys.shape, BF16),
            pltpu.VMEM(queries.shape, BF16),
            pltpu.VMEM((qpk, tok, tok), F32),
            pltpu.VMEM((tok, T * dh), BF16),
            pltpu.VMEM((dw // T, T * dh), BF16),
            pltpu.VMEM((dw, dh), BF16),
            pltpu.VMEM((2, codes, rows // 2, dh), BF16),
            pltpu.VMEM((2, codes, rows // 2, dh), BF16),
            pltpu.VMEM((2, codes, rows // 2, dh), BF16),
            dma((6,)),
            dma((2, G)), dma((2, G)),
            dma((2, codes)), dma((2, T, G // T)),
            dma((2, G // T // 2, T, 2 << fold)), dma((2, G // T // 2, T, 2 << fold)),
            dma((T,)), dma((T,)),
            dma((2, codes)), dma((2, codes)),
            dma((2, codes)), dma((2, codes)),
        ],
        compiler_params=pltpu.CompilerParams(
            collective_id=0, has_side_effects=True, vmem_limit_bytes=40 * 1024 * 1024),
    )(*[pltpu.with_memory_space_constraint(x, pltpu.HBM) for x in (hidden, w_value, queries, keys, out_grad, lengths)])
    count = len(results)
    return pl.pallas_call(
        functools.partial(put_out, count),
        out_shape=tuple(sds(x.shape, x.dtype) for x in results),
        in_specs=[pl.BlockSpec(memory_space=pltpu.VMEM)] * count,
        out_specs=(hbm,) * count,
        scratch_shapes=[dma((count,))],
        compiler_params=pltpu.CompilerParams(vmem_limit_bytes=8 * 1024 * 1024),
    )(*results)


def solution(mesh):
    row, both = P("group", None), P("group", "tensor")
    return jax.shard_map(
        functools.partial(per_device, mesh.shape["group"], mesh.shape["tensor"]),
        mesh=mesh,
        in_specs=(row, both, both, both, both, row),
        out_specs=(both,) * 5,
        check_vma=False,
    )
```
